32 devices in a mesh: groups: 2 (over x), tm: 16 (over z, y, core).
Axes of the slice: x: 2, y: 2, z: 4, core: 2. Of those that a mesh axis runs over, the one named last changes fastest.
Arguments:
- latent: bfloat16 [8192, 1536], P(('groups', 'tm')), parts along dimension 0, may hold values from -6 to 6
- entering: bfloat16 [512, 1536], P('groups'), parts along dimension 0, may hold values from -6 to 6
- qkv_weight: bfloat16 [1536, 4608], P('tm'), may hold values from -0.15625 to 0.15625
- modulation: float32 [256, 3, 1536], replicated, may hold values from -1.5 to 7, as said below
- levels: int32 [4, 16], P('groups'), parts along dimension 0, may hold values from 0 to 255
- offset: int32 [2], P('groups'), parts along dimension 0, may hold values from 0 to 15
Outputs:
- latent_next: bfloat16 [8192, 1536], P(('groups', 'tm')), parts along dimension 0
The draws below stay inside these ranges and needn't reach their ends.
There are 2 independent parts, one for each index of `groups`. The reference program is written for one: setup_inputs(seed, part) draws one part's arguments, and reference() takes and returns one part's arrays. A program takes and returns all parts, laid end to end along the dimension named above; an argument that names none is the same for every part. Nothing has to cross between parts.
Inputs may be any that keep to these rules, and one draw needn't show every extreme that they name: `modulation`: columns 0 and 1 hold a level's shift and scale, column 2 its gate, which is positive.
All inputs are finite; a program needn't handle non-finite values.
Results may differ from the reference program's by a relative error of at most 0.02.
The reference program's roundings to bfloat16 on the way count: a program that leaves them out, or rounds other values in their place, can miss the bound.
Values may be sent and summed in bfloat16 or wider, within the bound.
No kernel may reach another device: no remote copies, remote signals or barrier semaphores. Data moves between devices by JAX's collectives and lax.ppermute only.
A program may use at most 128 MiB of HBM per device.

```python
import jax
import jax.numpy as jnp
from jax import lax

HEADS = 12
HEAD = 128
DW = 1536
TOK = 256
LEVELS = 256
RADIUS = 2
SLABS = 16
ROWS = 4096
N_TM = 16


def draw_modulation(key, part):
    key_shift, key_scale, key_gate = jax.random.split(key, 3)
    shift = jnp.clip(0.5 * jax.random.normal(key_shift, (LEVELS, DW), jnp.float32), -1.5, 1.5)
    scale = jax.random.uniform(key_scale, (LEVELS, DW), jnp.float32, -0.5, 1.0)
    gate = jnp.exp(jax.random.uniform(key_gate, (LEVELS, DW), jnp.float32, 0.0, jnp.log(6.0)))
    return jnp.stack([shift, scale, gate], axis=1)


def with_ends(result, key, smallest, largest):
    extent = result.shape
    index_at = [jax.random.randint(jax.random.fold_in(key, axis), (), 0, extent[axis]) for axis in range(len(extent))]
    result = result.at[tuple(index_at)].set(smallest)
    longest = extent.index(max(extent))
    index_at[longest] = (index_at[longest] + 1) % extent[longest]
    return result.at[tuple(index_at)].set(largest)


def block_levels(key, dims, pieces, low, high):
    factor_of, own = 1.0, jax.random.fold_in(key, 6)
    for dim, blocks in pieces:
        draws = jnp.exp(jax.random.uniform(jax.random.fold_in(own, dim), (blocks,), jnp.float32, low / len(pieces), high / len(pieces)))
        factor_of = factor_of * jnp.repeat(draws, dims[dim] // blocks).reshape([-1 if axis == dim else 1 for axis in range(len(dims))])
    return factor_of


def scatter_about(key, extent, width, bound, pieces=(), kind=jnp.bfloat16):
    level = block_levels(key, extent, pieces, -0.22, 0.18) if pieces else 1.0
    values = jax.random.normal(key, extent, jnp.float32) * width * level
    return jnp.minimum(jnp.maximum(values, -bound), bound).astype(kind)


def setup_inputs(seed: int = 0, part: int = 0) -> dict:
    key_of = jax.random.split(jax.random.key(seed), 7)
    part_splits = jax.random.split(jax.random.fold_in(key_of[6], part), 7)
    return {
        "latent": scatter_about(part_splits[0], (ROWS, DW), 1.0, 6.0, ((0, 16),)),
        "entering": scatter_about(part_splits[1], (TOK, DW), 1.0, 6.0),
        "qkv_weight": scatter_about(key_of[2], (DW, 3 * DW), DW ** -0.5, 0.15625, ((0, 16),)),
        "modulation": draw_modulation(jax.random.fold_in(key_of[6], 71), part),
        "levels": with_ends(jax.random.randint(part_splits[4], (2, SLABS), 0, LEVELS), jax.random.fold_in(part_splits[4], 1), 0, LEVELS - 1).astype(jnp.int32),
        "offset": jax.random.randint(part_splits[5], (1,), 0, SLABS).astype(jnp.int32),
    }


def denoise(state, level_row, qkv_weight, modulation):
    slab_count = state.shape[0]
    tok_count = state.shape[1]
    channels = state.shape[2]
    state_f = state.astype(jnp.float32)
    normed = state_f * lax.rsqrt(lax.optimization_barrier(jnp.mean(state_f * state_f, axis=-1, keepdims=True)) + 1e-06)
    table = modulation[level_row]
    inputs = (normed * (1.0 + table[:, 1][:, None, :]) + table[:, 0][:, None, :]).astype(jnp.bfloat16)
    projected = jnp.dot(inputs.reshape(slab_count * tok_count, channels), qkv_weight, preferred_element_type=jnp.float32)
    projected = projected.astype(jnp.bfloat16).reshape(slab_count, tok_count, 3 * channels)
    queries = projected[:, :, :channels]
    key_value = projected[:, :, channels:]
    padding = jnp.zeros((RADIUS, tok_count, 2 * channels), jnp.bfloat16)
    padded = jnp.concatenate([padding, key_value, padding], axis=0)

    def one_slab(index):
        block = lax.dynamic_slice_in_dim(padded, index, 2 * RADIUS + 1, 0).reshape(-1, 2 * channels)
        heads_q = lax.dynamic_index_in_dim(queries, index, 0, keepdims=False).reshape(tok_count, HEADS, HEAD).astype(jnp.float32)
        key_block = block[:, :channels].reshape(-1, HEADS, HEAD).astype(jnp.float32)
        value_block = block[:, channels:].reshape(-1, HEADS, HEAD).astype(jnp.float32)
        scores = jnp.einsum('qhd,khd->hqk', heads_q, key_block) * HEAD ** (-0.5)
        key_slot = index - RADIUS + jnp.arange(block.shape[0], dtype=jnp.int32) // tok_count
        usable = (key_slot >= 0) & (key_slot < slab_count)
        masked = jnp.where(usable[None, None, :], scores, -jnp.inf)
        row_max = lax.optimization_barrier(jnp.max(masked, axis=-1, keepdims=True))
        exp_terms = jnp.where(usable[None, None, :], jnp.exp(masked - row_max), 0.0)
        weights = (exp_terms / lax.optimization_barrier(jnp.sum(exp_terms, axis=-1, keepdims=True))).astype(jnp.bfloat16)
        mixed = jnp.einsum('hqk,khd->qhd', weights.astype(jnp.float32), value_block)
        return mixed.reshape(tok_count, channels)
    mixed = lax.map(one_slab, jnp.arange(slab_count, dtype=jnp.int32))
    return (state_f + table[:, 2][:, None, :] * mixed).astype(jnp.bfloat16)

def reference(latent, entering, qkv_weight, modulation, levels, offset):
    slab_count = N_TM
    blocks = latent.reshape(slab_count, TOK, -1)
    slot_order = jnp.mod(jnp.arange(slab_count, dtype=jnp.int32) + offset[0], slab_count).astype(jnp.int32)
    state = blocks[slot_order]
    first = denoise(state, levels[0], qkv_weight, modulation)
    rolled = jnp.concatenate([first[1:], entering[None]], axis=0)
    second = denoise(rolled, levels[1], qkv_weight, modulation)
    placing = jnp.mod(jnp.arange(slab_count, dtype=jnp.int32) - offset[0] - 1, slab_count).astype(jnp.int32)
    return second[placing].reshape(slab_count * TOK, -1)
```

```python
import functools

import jax
import jax.numpy as jnp
from jax import lax
from jax.experimental import pallas as pl
from jax.experimental.pallas import tpu as pltpu
from jax.sharding import PartitionSpec as P

HEAD = 128
RADIUS = 2
BOTH = ("groups", "tm")


def plane_size(mesh):
    try:
        line = mesh.devices.reshape(mesh.devices.shape)[0]
        count = 1
        while count < len(line) and line[count].coords[2] == line[0].coords[2]:
            count += 1
        return count
    except AttributeError:
        return 2


class Place:
    def __init__(self, mesh):
        self.groups = mesh.shape["groups"]
        self.n = mesh.shape["tm"]
        self.plane = plane_size(mesh)
        self.planes = self.n // self.plane
        self.square = self.groups == 2 and self.plane == 4 and 2 < self.planes <= 8

    def move(self, value, where):
        pairs = []
        for group in range(self.groups):
            for t in range(self.n):
                to_group, to = where(group, t)
                pairs.append((group * self.n + t, to_group * self.n + to % self.n))
        return lax.ppermute(value, BOTH, pairs)

    def core(self, value):
        return self.move(value, lambda g, t: (g, t ^ 1))

    def across_y(self, value):
        return self.move(value, lambda g, t: (g, t ^ 2))

    def across_x(self, value):
        return self.move(value, lambda g, t: (1 - g, t))

    def along_z(self, value):
        return self.move(value, lambda g, t: (g, t + self.plane))

    def onward(self, value):
        return self.move(value, lambda g, t: (g, t + self.plane if t % 4 < 2 else t - self.plane))


def chip_of(place, t):
    first = t - lax.rem(t, 2)
    n = place.n
    ahead, behind = lax.rem(first + 2, n), lax.rem(first + n - 2, n)
    if not place.square:
        return behind, ahead, False
    even = lax.rem(t, 4) < 2
    return jnp.where(even, ahead, behind), jnp.where(even, behind, ahead), even


def gather_weight(place, qkv_weight, width):
    group, t = lax.axis_index("groups"), lax.axis_index("tm")
    core = lax.rem(t, 2)
    half = width // 2

    def half_of(which):
        return jnp.concatenate(
            [lax.dynamic_slice_in_dim(qkv_weight, part * width + which * half, half, 1) for part in range(3)], axis=1
        )

    mine = half_of(core)
    if not place.square:
        return [lax.all_gather(qkv_weight, "tm", axis=0, tiled=True)]
    partner = place.core(half_of(1 - core))
    unit = jnp.where(core == group, mine, partner)
    spare = jnp.where(core == group, partner, mine)
    pieces = [unit, spare]
    over = place.across_y(unit)
    pieces += [over, place.across_x(over)]
    ring = unit
    for step in range(1, place.planes):
        ring = place.along_z(ring)
        side = place.across_x(ring)
        over = place.across_y(ring)
        corner = place.across_y(side) if step == 1 else place.across_x(over)
        pieces += [ring, side, over, corner]
    return pieces


def piece_row(place, number, group, t):
    z, y = t // place.plane, lax.rem(t, place.plane) // 2
    step, which = number // 4, number % 4
    z = lax.rem(z + place.planes - step, place.planes)
    unit = group
    if step == 0:
        unit = 1 - group if which % 2 else group
    else:
        unit = 1 - group if which in (1, 3) else group
    if which >= 2:
        y = 1 - y
    return z * place.plane + y * 2 + unit


def step_kernel(place, late, count, offset_ref, *refs):
    slabs = refs[:6]
    pieces = refs[6 : 6 + count]
    out_ref, weight, u_all, queries, keys, values, sems = refs[6 + count :]
    group, t = lax.axis_index("groups"), lax.axis_index("tm")
    core = lax.rem(t, 2)
    tok = u_all.shape[1]
    half = queries.shape[-1]
    rows = weight.shape[0] // count
    copies = []
    for number, slab in enumerate(slabs):
        copies.append(pltpu.make_async_copy(slab, u_all.at[number], sems.at[number]))
    if count == 1:
        width = 2 * half
        for part in range(3):
            start = pl.multiple_of(part * width + core * half, 128)
            copies.append(
                pltpu.make_async_copy(
                    pieces[0].at[:, pl.ds(start, half)], weight.at[:, part * half : (part + 1) * half], sems.at[6 + part]
                )
            )
    else:
        for number, piece in enumerate(pieces):
            row = pl.multiple_of(piece_row(place, number, group, t) * rows, 16)
            copies.append(pltpu.make_async_copy(piece, weight.at[pl.ds(row, rows), :], sems.at[6 + number]))
    for copy in copies:
        copy.start()
    for copy in copies:
        copy.wait()

    block = 256

    def project(slab, carry):
        u = u_all[slab]
        for start in range(half, 3 * half, block):
            part = jnp.dot(u, weight[:, start : start + block], preferred_element_type=jnp.float32).astype(jnp.bfloat16)
            if start < 2 * half:
                keys[slab, :, start - half : start - half + block] = part
            else:
                values[slab, :, start - 2 * half : start - 2 * half + block] = part
        return carry

    def ask(slab, carry):
        u = u_all[slab]
        for start in range(0, half, block):
            queries[slab, :, start : start + block] = jnp.dot(
                u, weight[:, start : start + block], preferred_element_type=jnp.float32
            ).astype(jnp.bfloat16)
        return carry

    lax.fori_loop(0, 2, ask, 0)
    lax.fori_loop(0, 6, project, 0)

    n = place.n
    first_chip, second_chip, first_is_next = chip_of(place, t)
    chip = t - core
    at_next = jnp.where(first_is_next, 2, 4)
    at_prev = 6 - at_next
    next_chip = jnp.where(first_is_next, first_chip, second_chip)
    prev_chip = jnp.where(first_is_next, second_chip, first_chip)
    slot_of = lambda device: lax.rem(device + 2 * n - offset_ref[0] - late, n)
    constant = 1.4426950408889634 * HEAD ** (-0.5)

    def attend(number, carry):
        which, head = number // (half // HEAD), lax.rem(number, half // HEAD)
        own = jnp.where(which == 0, core, 1 - core)
        slot = slot_of(chip + own)
        columns = pl.ds(pl.multiple_of(head * HEAD, HEAD), HEAD)
        far_core = own
        places = [
            (jnp.int32(0), chip + core),
            (jnp.int32(1), chip + 1 - core),
            (at_next + jnp.where(core == 0, 0, 1), next_chip),
            (at_prev + jnp.where(core == 1, 0, 1), prev_chip + 1),
            (
                jnp.where(own == 0, at_prev, at_next) + jnp.where(core == far_core, 0, 1),
                jnp.where(own == 0, prev_chip, next_chip) + far_core,
            ),
        ]
        query = queries[which, :, columns]
        scores, tops, biases = [], [], []
        for spot, device in places:
            key = keys[spot, :, columns]
            score = lax.dot_general(query, key, (((1,), (1,)), ((), ())), preferred_element_type=jnp.float32)
            away = jnp.abs(slot_of(device) - slot)
            bias = jnp.where(away <= RADIUS, 0.0, -jnp.inf).astype(jnp.float32)
            scores.append(score)
            biases.append(bias)
            tops.append(jnp.max(score, axis=1, keepdims=True) + bias)
        top = functools.reduce(jnp.maximum, tops) * constant
        total, mixed = None, None
        for (spot, device), score, bias in zip(places, scores, biases):
            weights = jnp.exp2(score * constant + (bias - top))
            row_sum = jnp.sum(weights, axis=1, keepdims=True)
            part = jnp.dot(weights.astype(jnp.bfloat16), values[spot, :, columns], preferred_element_type=jnp.float32)
            total = row_sum if total is None else total + row_sum
            mixed = part if mixed is None else mixed + part
        out_ref[which, :, columns] = (mixed / total).astype(jnp.bfloat16)
        return carry

    lax.fori_loop(0, 2 * (half // HEAD), attend, 0)


def step(place, late, offset, slabs, pieces):
    tok, width = slabs[0].shape
    half = width // 2
    anywhere = pl.BlockSpec(memory_space=pl.ANY)
    return pl.pallas_call(
        functools.partial(step_kernel, place, late, len(pieces)),
        out_shape=jax.ShapeDtypeStruct((2, tok, half), jnp.bfloat16),
        in_specs=[pl.BlockSpec(memory_space=pltpu.SMEM)] + [anywhere] * (len(slabs) + len(pieces)),
        out_specs=pl.BlockSpec(memory_space=pltpu.VMEM),
        scratch_shapes=[
            pltpu.VMEM((width, 3 * half), jnp.bfloat16),
            pltpu.VMEM((6, tok, width), jnp.bfloat16),
            pltpu.VMEM((2, tok, half), jnp.bfloat16),
            pltpu.VMEM((6, tok, half), jnp.bfloat16),
            pltpu.VMEM((6, tok, half), jnp.bfloat16),
            pltpu.SemaphoreType.DMA((6 + max(3, len(pieces)),)),
        ],
        compiler_params=pltpu.CompilerParams(vmem_limit_bytes=48 << 20),
        cost_estimate=pl.CostEstimate(flops=10**10, bytes_accessed=15 * 10**6, transcendentals=4 * 10**6),
        name="step%d" % late,
    )(offset, *slabs, *pieces)


def modulate(state, level, modulation):
    state_f = state.astype(jnp.float32)
    normed = state_f * lax.rsqrt(jnp.mean(state_f * state_f, axis=-1, keepdims=True) + 1e-06)
    table = lax.dynamic_index_in_dim(modulation, level, 0, keepdims=False)
    return (normed * (1.0 + table[1]) + table[0]).astype(jnp.bfloat16), table[2]


def spread(place, u):
    if place.square:
        first = place.across_y(u)
        second = place.onward(first)
    else:
        first = place.move(u, lambda g, t: (g, t + 2))
        second = place.move(u, lambda g, t: (g, t - 2))
    return [u, place.core(u), first, place.core(first), second, place.core(second)]


def finish(place, state, gate, mixed):
    core = lax.rem(lax.axis_index("tm"), 2)
    own, other = mixed[0], place.core(mixed[1])
    whole = jnp.concatenate([jnp.where(core == 0, own, other), jnp.where(core == 0, other, own)], axis=1)
    return (state.astype(jnp.float32) + gate * whole.astype(jnp.float32)).astype(jnp.bfloat16)


def local(place, latent, entering, qkv_weight, modulation, levels, offset):
    n = place.n
    slot = jnp.mod(lax.axis_index("tm") - offset[0], n)
    u, gate = modulate(latent, levels[0, slot], modulation)
    slabs = spread(place, u)
    pieces = gather_weight(place, qkv_weight, latent.shape[1])
    mixed = step(place, 0, offset, slabs, pieces)
    first = finish(place, latent, gate, mixed)
    state = jnp.where(slot == 0, entering, first)
    u, gate = modulate(state, levels[1, jnp.mod(slot - 1, n)], modulation)
    slabs = spread(place, u)
    mixed = step(place, 1, offset, slabs, pieces)
    return finish(place, state, gate, mixed)


def solution(mesh):
    place = Place(mesh)
    placed = (
        P(BOTH, None),
        P("groups", None),
        P("tm", None),
        P(),
        P("groups", None),
        P("groups"),
    )
    return jax.shard_map(
        functools.partial(local, place), mesh=mesh, in_specs=placed, out_specs=P(BOTH, None), check_vma=False
    )
```
